1024 devices in a mesh: dom: 2 (over core), gx: 32 (over y, z_hi), gy: 16 (over z_lo, x).
Axes of the slice: x: 4, y: 8, z: 16 (z_hi: 4, z_lo: 4; z = z_hi * 4 + z_lo), core: 2. Of those that a mesh axis runs over, the one named last changes fastest.
Arguments:
- wind: float32 [2, 3, 512, 256, 128], P('dom', None, 'gx', 'gy'), may hold values from -6 to 6
- adjoint: float32 [2, 4, 512, 256, 128], P('dom', None, 'gx', 'gy'), may hold values from -6 to 6
- turbines: int32 [512, 256, 128], P('gx', 'gy'), may hold values 0 or 1
- fringe_range: int32 [2], replicated, may hold values from 64 to 511, as said below
Outputs:
- earlier: float32 [2, 4, 512, 256, 128], P('dom', None, 'gx', 'gy')
The draws below stay inside these ranges and needn't reach their ends.
Inputs may be any that keep to these rules, and one draw needn't show every extreme that they name: `fringe_range`: element 0 is the first streamwise cell of the fringe, the last cell 512 - 1 of the domain, and element 1 its length in cells, from 64 to 128; the fringe wraps around the periodic streamwise dimension.
All inputs are finite; a program needn't handle non-finite values. No bound on the sum of `turbines` on one device may be relied on, other than what follows from the above.
Results may differ from the reference program's by a relative error of at most 0.00002.
Values sent between devices are 32-bit elements; how exact they have to be, the bound alone decides.
No kernel may reach another device: no remote copies, remote signals or barrier semaphores. Data moves between devices by JAX's collectives and lax.ppermute only.
A program may use at most 32 MiB of HBM per device.

```python
import math
import jax
import jax.numpy as jnp

STEPS = 2
NX = 512
NY = 256
NZ = 128


def draw_fringe_range(key, part):
    span_key = jax.random.fold_in(key, 17)
    fringe_span = jax.random.randint(span_key, (1,), NX // 8, NX // 4 + 1)
    first_cell = jnp.full((1,), NX - 1, dtype=jnp.int32)
    return jnp.concatenate([first_cell, fringe_span.astype(jnp.int32)]).astype(jnp.int32)


def set_ends(entries, key, least, top_value):
    shape = entries.shape
    spot = [jax.random.randint(jax.random.fold_in(key, axis), (), 0, shape[axis]) for axis in range(len(shape))]
    entries = entries.at[tuple(spot)].set(least)
    longest = shape.index(max(shape))
    spot[longest] = (spot[longest] + 1) % shape[longest]
    return entries.at[tuple(spot)].set(top_value)


def level_of(rng, shape, cuts, least, top_value):
    def one(dim, parts):
        draws = jax.random.uniform(jax.random.fold_in(jax.random.fold_in(rng, 6), dim), (parts,), jnp.float32, least / len(cuts), top_value / len(cuts))
        return jnp.repeat(jnp.exp(draws), shape[dim] // parts).reshape((-1,) + (1,) * (len(shape) - dim - 1))

    factor_of = one(*cuts[0])
    for cut in cuts[1:]:
        factor_of = factor_of * one(*cut)
    return factor_of


def noise(rng, dims, width, reach, cuts=(), kind=jnp.bfloat16):
    factor_of = level_of(rng, dims, cuts, -0.22, 0.18) if cuts else 1.0
    result = jax.random.normal(rng, dims, jnp.float32) * width * factor_of
    return jnp.minimum(jnp.maximum(result, -reach), reach).astype(kind)


def setup_inputs(seed: int = 0) -> dict:
    key_of = jax.random.split(jax.random.key(seed), 5)
    wind = noise(key_of[0], (2, 3, NX, NY, NZ), 1.0, 6.0, ((0, 2), (2, 32), (3, 16)), jnp.float32)
    adjoint = noise(key_of[1], (2, 4, NX, NY, NZ), 1.0, 6.0, ((0, 2), (2, 32), (3, 16)), jnp.float32)
    turbines = set_ends((jax.random.randint(key_of[2], (NX, NY, NZ), 0, 8) < 1).astype(jnp.int32), jax.random.fold_in(key_of[2], 1), 0, 1)
    fringe_range = draw_fringe_range(jax.random.fold_in(key_of[4], 71), 0)
    return {"wind": wind, "adjoint": adjoint, "turbines": turbines, "fringe_range": fringe_range}


DT = 0.1
SMAG = 0.1
SOUND_SQ = 4.0
DRAG = 1.0
RATE = 3.0

def crop_xy(field, margin):
    if margin == 0:
        return field
    return field[..., margin:field.shape[-3] - margin, margin:field.shape[-2] - margin, :]

def pad_z(field):
    return jnp.pad(field, [(0, 0)] * (field.ndim - 1) + [(1, 1)])

def diff_x(field):
    return 0.5 * (field[..., 2:, 1:-1, :] - field[..., :-2, 1:-1, :])

def diff_y(field):
    return 0.5 * (field[..., 1:-1, 2:, :] - field[..., 1:-1, :-2, :])

def diff_z(field):
    padded = crop_xy(pad_z(field), 1)
    return 0.5 * (padded[..., 2:] - padded[..., :-2])

def eddy(wind_ext):
    grads = (diff_x(wind_ext), diff_y(wind_ext), diff_z(wind_ext))
    strain_sq = jnp.zeros_like(grads[0][0])
    for first in range(3):
        for second in range(3):
            strain = 0.5 * (grads[first][second] + grads[second][first])
            strain_sq = strain_sq + strain * strain
    return SMAG * jnp.sqrt(2.0 * strain_sq)

def spread(field, viscosity):
    centre = crop_xy(field, 1)
    visc_mid = crop_xy(viscosity, 1)
    flux_xp = (viscosity[..., 2:, 1:-1, :] + visc_mid) * 0.5 * (field[..., 2:, 1:-1, :] - centre)
    flux_xm = (visc_mid + viscosity[..., :-2, 1:-1, :]) * 0.5 * (centre - field[..., :-2, 1:-1, :])
    flux_yp = (viscosity[..., 1:-1, 2:, :] + visc_mid) * 0.5 * (field[..., 1:-1, 2:, :] - centre)
    flux_ym = (visc_mid + viscosity[..., 1:-1, :-2, :]) * 0.5 * (centre - field[..., 1:-1, :-2, :])
    visc_pad = pad_z(visc_mid)
    field_pad = pad_z(centre)
    flux_zp = (visc_pad[..., 2:] + visc_mid) * 0.5 * (field_pad[..., 2:] - centre)
    flux_zm = (visc_mid + visc_pad[..., :-2]) * 0.5 * (centre - field_pad[..., :-2])
    return flux_xp - flux_xm + flux_yp - flux_ym + flux_zp - flux_zm

def tendency(adjoint_ext, wind_here, viscosity, drag_cells):
    along_x = diff_x(adjoint_ext)
    along_y = diff_y(adjoint_ext)
    along_z = diff_z(adjoint_ext)
    advection = wind_here[0] * along_x + wind_here[1] * along_y + wind_here[2] * along_z
    diffusion = spread(adjoint_ext[:3], viscosity)
    wind_speed = jnp.sqrt(wind_here[0] * wind_here[0] + wind_here[1] * wind_here[1] + wind_here[2] * wind_here[2])
    centre = crop_xy(adjoint_ext, 1)
    acoustic = SOUND_SQ * jnp.stack([along_x[3], along_y[3], along_z[3]], 0)
    velocity = advection[:3] + diffusion + acoustic - DRAG * drag_cells * wind_speed * centre[:3]
    pressure = advection[3] + along_x[0] + along_y[1] + along_z[2]
    return (centre, jnp.concatenate([velocity, pressure[None]], 0))

def ramp(position, fringe_range, length_total):
    offset = jnp.mod(position - fringe_range[0], length_total)
    fringe_width = fringe_range[1]
    fringe_phase = math.pi * (offset.astype(jnp.float32) + 0.5) / fringe_width.astype(jnp.float32)
    sine = jnp.sin(fringe_phase)
    return jnp.where(offset < fringe_width, RATE * sine * sine, 0.0).astype(jnp.float32)

def wrap_xy(field, extent):
    return jnp.pad(field, [(0, 0)] * (field.ndim - 3) + [(extent, extent), (extent, extent), (0, 0)], mode='wrap')

def reference(wind, adjoint, turbines, fringe_range):
    fringe_rates = ramp(jnp.arange(NX, dtype=jnp.int32), fringe_range, NX)[:, None, None]
    drag_main = turbines.astype(jnp.float32)
    nothing = jnp.zeros_like(drag_main)
    viscosity = [eddy(wrap_xy(wind[domain], 1)) for domain in range(2)]
    states = [adjoint[0], adjoint[1]]
    for step in range(STEPS):
        updated = []
        forcing = None
        for domain in range(2):
            drag_cells = drag_main if domain == 0 else nothing
            centre, rate_term = tendency(wrap_xy(states[domain], 1), wind[domain], wrap_xy(viscosity[domain], 1), drag_cells)
            if domain == 0:
                forcing = jnp.concatenate([fringe_rates * centre[:3], jnp.zeros_like(centre[3:])], 0)
                updated.append(centre + DT * (rate_term - forcing))
            else:
                updated.append(centre + DT * (rate_term + forcing))
        states = updated
    return jnp.stack(states)
```

```python
import functools
import math

import jax
import jax.numpy as jnp
from jax import lax
from jax.experimental import pallas as pl
from jax.experimental.pallas import tpu as pltpu
from jax.sharding import PartitionSpec as P

DT = 0.1
SMAG = 0.1
SOUND_SQ = 4.0
DRAG = 1.0
RATE = 3.0

T = 16
NZ = 128
R = 24
F32 = jnp.float32
VMEM = pl.BlockSpec(memory_space=pltpu.VMEM)
SMEM = pl.BlockSpec(memory_space=pltpu.SMEM)

Y_WIND, Y_ADJ, Y_DRAG, Y_LEN = 0, 9, 17, 18
X_U1, X_U2, X_A1, X_A2, X_NU2, X_D1, X_LEN = 0, 60, 114, 186, 250, 266, 288


def shape(*dims):
    return jax.ShapeDtypeStruct(dims, F32)


def call(body, outs, n_in, scratch=(), specs=None):
    return pl.pallas_call(
        body,
        out_shape=outs,
        in_specs=[VMEM] * n_in if specs is None else specs,
        out_specs=jax.tree.map(lambda _: VMEM, outs),
        scratch_shapes=[pltpu.VMEM(s, F32) for s in scratch],
    )


def is_main():
    return (lax.axis_index("dom") == 0).astype(F32)


def up_z(v):
    return pltpu.roll(v, NZ - 1, 1)


def down_z(v):
    return pltpu.roll(v, 1, 1)


def edges_z(rows):
    lane = lax.broadcasted_iota(jnp.int32, (rows, NZ), 1)
    return (lane < NZ - 1).astype(F32), (lane > 0).astype(F32)


def drag_rows(u, v, w, turb):
    return (DT * DRAG) * turb * jnp.sqrt(u * u + v * v + w * w) * is_main()


def pack_y(w, a, t, up, dn):
    for msg, edge in ((up, T - 3), (dn, 0)):
        near = 0 if edge == 0 else T - 1
        for c in range(3):
            for l in range(3):
                msg[Y_WIND + 3 * c + l] = w[c, pl.ds(edge + l, T, stride=T), :]
        for c in range(4):
            for l in range(2):
                at = l if edge == 0 else T - 2 + l
                msg[Y_ADJ + 2 * c + l] = a[c, pl.ds(at, T, stride=T), :]
        u, v, z = (w[c, pl.ds(near, T, stride=T), :] for c in range(3))
        turb = t[pl.ds(near, T, stride=T), :].astype(F32)
        msg[Y_DRAG] = drag_rows(u, v, z, turb)


def nu_row(ew, base, at, ones_p, ones_m, rows=R):
    g = []
    for c in range(3):
        mid = ew[c, pl.ds(at, rows), :]
        gx = ew[c, pl.ds(at + R, rows), :] - ew[c, pl.ds(at - R, rows), :]
        gy = ew[c, pl.ds(at + 1, rows), :] - ew[c, pl.ds(at - 1, rows), :]
        gz = up_z(mid) * ones_p - down_z(mid) * ones_m
        g.append((gx, gy, gz))
    diag = g[0][0] * g[0][0] + g[1][1] * g[1][1] + g[2][2] * g[2][2]
    xy = g[1][0] + g[0][1]
    xz = g[2][0] + g[0][2]
    yz = g[2][1] + g[1][2]
    return SMAG * jnp.sqrt(0.5 * diag + 0.25 * (xy * xy + xz * xz + yz * yz))


def pack_x(w, a, t, lo, hi, up, dn, ew, ea, ed):
    for c in range(3):
        for x in range(T):
            ew[c, pl.ds(x * R + 3, T), :] = w[c, pl.ds(x * T, T), :]
        for l in range(3):
            ew[c, pl.ds(l, T, stride=R), :] = lo[Y_WIND + 3 * c + l]
            ew[c, pl.ds(T + 3 + l, T, stride=R), :] = hi[Y_WIND + 3 * c + l]
    for c in range(4):
        for x in range(T):
            ea[c, pl.ds(x * R + 3, T), :] = a[c, pl.ds(x * T, T), :]
        for l in range(2):
            ea[c, pl.ds(1 + l, T, stride=R), :] = lo[Y_ADJ + 2 * c + l]
            ea[c, pl.ds(T + 3 + l, T, stride=R), :] = hi[Y_ADJ + 2 * c + l]
    main = is_main()
    for x in range(T):
        u, v, z = (w[c, pl.ds(x * T, T), :] for c in range(3))
        turb = t[pl.ds(x * T, T), :].astype(F32)
        ed[pl.ds(x * R + 3, T), :] = drag_rows(u, v, z, turb)
    ed[pl.ds(2, T, stride=R), :] = lo[Y_DRAG]
    ed[pl.ds(T + 3, T, stride=R), :] = hi[Y_DRAG]
    ones_p, ones_m = edges_z(T)
    for msg, x1, x2 in ((up, T - 1, T - 2), (dn, 0, 1)):
        for c in range(3):
            msg[pl.ds(X_U1 + 20 * c, 20), :] = ew[c, pl.ds(x1 * R + 1, 20), :]
            msg[pl.ds(X_U2 + 18 * c, 18), :] = ew[c, pl.ds(x2 * R + 2, 18), :]
        for c in range(4):
            msg[pl.ds(X_A1 + 18 * c, 18), :] = ea[c, pl.ds(x1 * R + 2, 18), :]
            msg[pl.ds(X_A2 + 16 * c, 16), :] = ea[c, pl.ds(x2 * R + 3, 16), :]
        msg[pl.ds(X_NU2, 16), :] = nu_row(ew, 0, x2 * R + 3, ones_p, ones_m, 16)
        msg[pl.ds(X_D1, 16), :] = ed[pl.ds(x1 * R + 3, 16), :]
        msg[pl.ds(X_D1 + 16, 6), :] = jnp.zeros((6, NZ), F32)


def fringe_table(fringe, table, rows):
    total = T * lax.axis_size("gx")
    x = lax.broadcasted_iota(jnp.int32, (rows, NZ), 0) - 1
    place = lax.axis_index("gx") * T + x - fringe[0]
    offset = lax.rem(place + 2 * total, jnp.full_like(place, total))
    width = fringe[1]
    phase = (math.pi * (offset.astype(F32) + 0.5)) / jnp.full((rows, NZ), width, jnp.int32).astype(F32)
    sine = jnp.sin(phase)
    table[...] = jnp.where(offset < width, (DT * RATE) * (sine * sine), 0.0)


def stencil(a, at, step, rows, coefs, wind, ones_p, ones_m):
    c0, cxp, cxm, cyp, cym, czp, czm = coefs
    new, dx, dy, dz = [], [], [], []
    for c in range(4):
        mid = a[c, pl.ds(at, rows), :]
        xp, xm = a[c, pl.ds(at + step, rows), :], a[c, pl.ds(at - step, rows), :]
        yp, ym = a[c, pl.ds(at + 1, rows), :], a[c, pl.ds(at - 1, rows), :]
        zp, zm = up_z(mid), down_z(mid)
        if c < 3:
            new.append(c0 * mid + (cxp * xp + cxm * xm) + (cyp * yp + cym * ym) + (czp * zp + czm * zm))
        else:
            new.append(mid)
        dx.append(xp - xm)
        dy.append(yp - ym)
        dz.append(zp * ones_p - zm * ones_m)
    half = 0.5 * DT
    sound = half * SOUND_SQ
    new[0] = new[0] + sound * dx[3]
    new[1] = new[1] + sound * dy[3]
    new[2] = new[2] + sound * dz[3]
    u, v, w = wind
    new[3] = new[3] + half * (u * dx[3] + v * dy[3] + w * dz[3] + dx[0] + dy[1] + dz[2])
    return new


def first_step(w, a, d, lo, hi, main_a, fringe, a1, cf, sent, ew, ea, ed, nu, table):
    main = is_main()
    fringe_table(fringe, table, R)
    for c in range(3):
        ew[c, pl.ds(2 * R, T * R), :] = w[c]
    for c in range(4):
        ea[c, pl.ds(2 * R, T * R), :] = a[c]
    ed[pl.ds(R, T * R), :] = d[...]
    for msg, p1, p2 in ((lo, 1, 0), (hi, T + 2, T + 3)):
        for c in range(3):
            ew[c, pl.ds(p1 * R + 1, 20), :] = msg[pl.ds(X_U1 + 20 * c, 20), :]
            ew[c, pl.ds(p2 * R + 2, 18), :] = msg[pl.ds(X_U2 + 18 * c, 18), :]
        for c in range(4):
            ea[c, pl.ds(p1 * R + 2, 18), :] = msg[pl.ds(X_A1 + 18 * c, 18), :]
            ea[c, pl.ds(p2 * R + 3, 16), :] = msg[pl.ds(X_A2 + 16 * c, 16), :]
        nu[pl.ds(p2 * R + 3, 16), :] = (0.5 * DT) * msg[pl.ds(X_NU2, 16), :]
        ed[pl.ds((p1 - 1) * R + 3, 16), :] = msg[pl.ds(X_D1, 16), :]
    ones_p, ones_m = edges_z(R)

    def nu_plane(x, _):
        at = pl.multiple_of(x * R, 8)
        nu[pl.ds(at, R), :] = (0.5 * DT) * nu_row(ew, 0, at, ones_p, ones_m)
        return 0

    lax.fori_loop(1, T + 3, nu_plane, 0)

    def plane(x, _):
        at = pl.multiple_of((x + 1) * R, 8)
        out = pl.multiple_of(x * R, 8)
        wind = [ew[c, pl.ds(at, R), :] for c in range(3)]
        h = nu[pl.ds(at, R), :]
        hxp, hxm = nu[pl.ds(at + R, R), :], nu[pl.ds(at - R, R), :]
        hyp, hym = nu[pl.ds(at + 1, R), :], nu[pl.ds(at - 1, R), :]
        hzp, hzm = up_z(h) * ones_p, down_z(h) * ones_m
        rate = jnp.broadcast_to(table[pl.ds(x, 1), :], (R, NZ))
        half = 0.5 * DT
        lost = ed[pl.ds(out, R), :] + main * rate
        c0 = (1.0 - lost) - (6.0 * h + (hxp + hxm) + (hyp + hym) + (hzp + hzm))
        pu, pv, pw = (half * v for v in wind)
        coefs = (
            c0,
            h + hxp + pu,
            h + hxm - pu,
            h + hyp + pv,
            h + hym - pv,
            (h + hzp + pw) * ones_p,
            (h + hzm - pw) * ones_m,
        )
        new = stencil(ea, at, R, R, coefs, wind, ones_p, ones_m)
        for c in range(4):
            a1[c, pl.ds(out, R), :] = new[c]
        for k in range(7):
            cf[k, pl.ds(out, R), :] = coefs[k]
        return 0

    lax.fori_loop(0, T + 2, plane, 0)
    for c in range(3):
        for x, p in ((0, 1), (T + 1, T + 2)):
            sent[c, pl.ds(x * T, T), :] = ea[c, pl.ds(p * R + 3, T), :]

    def force(x, _):
        out = pl.multiple_of((x + 1) * R, 8)
        src = pl.multiple_of(x * R, 8)
        rate = jnp.broadcast_to(table[pl.ds(x + 1, 1), :], (R, NZ)) * (1.0 - main)
        for c in range(3):
            v = a1[c, pl.ds(out, R), :] + rate * main_a[c, pl.ds(src, R), :]
            a1[c, pl.ds(out, R), :] = v
        for c in range(3):
            sent[c, pl.ds(pl.multiple_of((x + 1) * T, 8), T), :] = a1[c, pl.ds(out + 3, T), :]
        return 0

    lax.fori_loop(0, T, force, 0)


def second_step(w, a1, cf, main_a, fringe, out, table):
    other = 1.0 - is_main()
    fringe_table(fringe, table, R)
    ones_p, ones_m = edges_z(T)

    def plane(x, _):
        at = (x + 1) * R + 3
        own = pl.multiple_of(x * T, 8)
        wind = [w[c, pl.ds(own, T), :] for c in range(3)]
        coefs = [cf[k, pl.ds(at, T), :] for k in range(7)]
        new = stencil(a1, at, R, T, coefs, wind, ones_p, ones_m)
        rate = jnp.broadcast_to(table[pl.ds(x + 1, 1), :], (T, NZ)) * other
        for c in range(3):
            new[c] = new[c] + rate * main_a[c, pl.ds(pl.multiple_of((x + 1) * T, 8), T), :]
        for c in range(4):
            out[c, pl.ds(own, T), :] = new[c]
        return 0

    lax.fori_loop(0, T, plane, 0)
    for x, p, k, sign in ((0, 0, 2, -1.0), (T - 1, T + 1, 1, 1.0)):
        rate = jnp.broadcast_to(table[pl.ds(p, 1), :], (T, NZ)) * other
        beside = [rate * main_a[c, pl.ds(p * T, T), :] for c in range(3)]
        coef = cf[k, pl.ds((x + 1) * R + 3, T), :]
        for c in range(3):
            out[c, pl.ds(x * T, T), :] = out[c, pl.ds(x * T, T), :] + coef * beside[c]
        out[3, pl.ds(x * T, T), :] = out[3, pl.ds(x * T, T), :] + (sign * 0.5 * DT) * beside[0]


def ring(axis, by):
    devices = lax.axis_size(axis)
    return [(i, (i + by) % devices) for i in range(devices)]


def on_device(wind, adjoint, turbines, fringe_range):
    w = wind.reshape(3, T * T, NZ)
    a = adjoint.reshape(4, T * T, NZ)
    t = turbines.reshape(T * T, NZ)
    y_msg = shape(Y_LEN, T, NZ)
    up, dn = call(pack_y, (y_msg, y_msg), 3)(w, a, t)
    lo = lax.ppermute(up, "gy", ring("gy", 1))
    hi = lax.ppermute(dn, "gy", ring("gy", -1))
    x_msg = shape(X_LEN, NZ)
    up, dn, ew, ea, ed = call(
        pack_x, (x_msg, x_msg, shape(3, T * R, NZ), shape(4, T * R, NZ), shape(T * R, NZ)), 5
    )(w, a, t, lo, hi)
    xlo = lax.ppermute(up, "gx", ring("gx", 1))
    xhi = lax.ppermute(dn, "gx", ring("gx", -1))
    main_a = lax.ppermute(ea, "dom", [(0, 1)])
    a1, cf, sent = call(
        first_step,
        (shape(4, (T + 2) * R, NZ), shape(7, (T + 2) * R, NZ), shape(3, (T + 2) * T, NZ)),
        7,
        scratch=(
            (3, (T + 4) * R, NZ),
            (4, (T + 4) * R, NZ),
            ((T + 2) * R, NZ),
            ((T + 4) * R, NZ),
            (R, NZ),
        ),
        specs=[VMEM] * 6 + [SMEM],
    )(ew, ea, ed, xlo, xhi, main_a, fringe_range)
    main_a1 = lax.ppermute(sent, "dom", [(0, 1)])
    out = call(second_step, shape(4, T * T, NZ), 5, scratch=((R, NZ),), specs=[VMEM] * 4 + [SMEM])(
        w, a1, cf, main_a1, fringe_range
    )
    return out.reshape(1, 4, T, T, NZ)


def solution(mesh):
    in_specs = (
        P("dom", None, "gx", "gy", None),
        P("dom", None, "gx", "gy", None),
        P("gx", "gy", None),
        P(),
    )
    out_specs = P("dom", None, "gx", "gy", None)
    return jax.shard_map(
        on_device, mesh=mesh, in_specs=in_specs, out_specs=out_specs, check_vma=False
    )
```

```python
import math

import jax
import jax.numpy as jnp
from jax import lax
from jax.experimental import pallas as pl
from jax.experimental.pallas import tpu as pltpu
from jax.sharding import PartitionSpec as P


DT = 0.1
HALF = 0.5 * DT
SMAG = 0.1
SOUND_SQ = 4.0
DRAG = 1.0
RATE = 3.0

T = 16
NZ = 128
R = 24
SPARE = 8
F32 = jnp.float32
VMEM = pl.BlockSpec(memory_space=pltpu.VMEM)
SMEM = pl.BlockSpec(memory_space=pltpu.SMEM)
HBM = pl.BlockSpec(memory_space=pltpu.HBM)

Y_WIND, Y_ADJ, Y_DRAG, Y_LEN = 0, 9, 17, 18
X_U1, X_U2, X_A1, X_A2, X_NU2, X_D1, X_LEN = 0, 60, 114, 186, 250, 266, 288
LEFT, RIGHT = 2, -8
KEPT = ((0, 1, 2), (13, 14, 15))


def shape(*dims):
    return jax.ShapeDtypeStruct(dims, F32)


def planes(n, *lead):
    return lead + (n * R + SPARE, NZ)


def call(body, outs, specs, scratch=(), flops=0):
    made = pl.pallas_call(
        body,
        out_shape=outs,
        in_specs=specs,
        out_specs=jax.tree.map(lambda _: VMEM, outs),
        scratch_shapes=scratch,
        compiler_params=pltpu.CompilerParams(vmem_limit_bytes=16 * 1024 * 1024),
        cost_estimate=pl.CostEstimate(flops=flops, bytes_accessed=0, transcendentals=0),
    )
    return made


def scratch(*dims):
    return pltpu.VMEM(dims, F32)


def is_main():
    return (lax.axis_index("dom") == 0).astype(F32)


def even(axis):
    return lax.rem(lax.axis_index(axis), 2) == 0


def up_z(v):
    return pltpu.roll(v, NZ - 1, 1)


def down_z(v):
    return pltpu.roll(v, 1, 1)


def edges_z(rows):
    lane = lax.broadcasted_iota(jnp.int32, (rows, NZ), 1)
    return (lane < NZ - 1).astype(F32), (lane > 0).astype(F32)


def drag_rows(u, v, w, turb):
    return (DT * DRAG) * turb * jnp.sqrt(u * u + v * v + w * w) * is_main()


def pack_y(w_hbm, a_hbm, t_hbm, first, second, w, a, t, sems):
    copies = [
        pltpu.make_async_copy(src, dst, sems.at[k])
        for k, (src, dst) in enumerate(((w_hbm, w), (a_hbm, a), (t_hbm, t)))
    ]
    for copy in copies:
        copy.start()
    sides = []
    for msg, top in ((first, even("gy")), (second, jnp.logical_not(even("gy")))):
        sides.append((msg, jnp.where(top, T - 3, 0), jnp.where(top, T - 2, 0), jnp.where(top, T - 1, 0)))
    copies[0].wait()
    for msg, edge, _, _ in sides:
        for c in range(3):
            for l in range(3):
                msg[Y_WIND + 3 * c + l] = w[c, pl.ds(edge + l, T, stride=T), :]
    copies[1].wait()
    for msg, _, edge, _ in sides:
        for c in range(4):
            for l in range(2):
                msg[Y_ADJ + 2 * c + l] = a[c, pl.ds(edge + l, T, stride=T), :]
    copies[2].wait()
    for msg, _, _, near in sides:
        u, v, z = (w[c, pl.ds(near, T, stride=T), :] for c in range(3))
        turb = t[pl.ds(near, T, stride=T), :].astype(F32)
        msg[Y_DRAG] = drag_rows(u, v, z, turb)


def y_rims(first, second, ew, ea, ed, shift, firsts, count):
    for msg, top in ((first, even("gy")), (second, jnp.logical_not(even("gy")))):
        base = (firsts + shift) * R
        at_w, at_a, at_d = (base + jnp.where(top, T + 3, k) for k in range(3))
        own = pl.ds(firsts, count)
        for c in range(3):
            for l in range(3):
                ew[c, pl.ds(at_w + l, count, stride=R), :] = msg[Y_WIND + 3 * c + l, own]
        for c in range(4):
            for l in range(2):
                ea[c, pl.ds(at_a + l, count, stride=R), :] = msg[Y_ADJ + 2 * c + l, own]
        ed[pl.ds(at_d, count, stride=R), :] = msg[Y_DRAG, own]


def own_rows(x, to, w, a, t, ew, ea, ed):
    wind = [w[c, pl.ds(x * T, T), :] for c in range(3)]
    for c in range(3):
        ew[c, pl.ds(to * R + 3, T), :] = wind[c]
    for c in range(4):
        ea[c, pl.ds(to * R + 3, T), :] = a[c, pl.ds(x * T, T), :]
    ed[pl.ds(to * R + 3, T), :] = drag_rows(*wind, t[pl.ds(x * T, T), :].astype(F32))


def spread_rows(w, a, t, first, second, ew, ea, ed, vel):
    for x in range(T):
        own_rows(x, x, w, a, t, ew, ea, ed)
    y_rims(first, second, ew, ea, ed, 0, 0, T)
    vel[...] = ea[pl.ds(0, 3), pl.ds(0, T * R), :]


def nu_rows(ew, at, rows, ones_p, ones_m):
    g = []
    for c in range(3):
        mid = ew[c, pl.ds(at, rows), :]
        gx = ew[c, pl.ds(at + R, rows), :] - ew[c, pl.ds(at - R, rows), :]
        gy = ew[c, pl.ds(at + 1, rows), :] - ew[c, pl.ds(at - 1, rows), :]
        gz = up_z(mid) * ones_p - down_z(mid) * ones_m
        g.append((gx, gy, gz))
    diag = g[0][0] * g[0][0] + g[1][1] * g[1][1] + g[2][2] * g[2][2]
    xy = g[1][0] + g[0][1]
    xz = g[2][0] + g[0][2]
    yz = g[2][1] + g[1][2]
    return SMAG * jnp.sqrt(0.5 * diag + 0.25 * (xy * xy + xz * xz + yz * yz))


def pack_x(w, a, t, first_y, second_y, first, second, ew, ea, ed):
    for x in KEPT[0] + KEPT[1]:
        own_rows(x, x if x < 8 else x - 10, w, a, t, ew, ea, ed)
    y_rims(first_y, second_y, ew, ea, ed, 0, 0, 3)
    y_rims(first_y, second_y, ew, ea, ed, -10, 13, 3)
    ones_p, ones_m = edges_z(T)
    for msg, top in ((first, even("gx")), (second, jnp.logical_not(even("gx")))):
        x1, x2 = jnp.where(top, 5 * R, 0), jnp.where(top, 4 * R, R)
        for c in range(3):
            msg[pl.ds(X_U1 + 20 * c, 20), :] = ew[c, pl.ds(x1 + 1, 20), :]
            msg[pl.ds(X_U2 + 18 * c, 18), :] = ew[c, pl.ds(x2 + 2, 18), :]
        for c in range(4):
            msg[pl.ds(X_A1 + 18 * c, 18), :] = ea[c, pl.ds(x1 + 2, 18), :]
            msg[pl.ds(X_A2 + 16 * c, 16), :] = ea[c, pl.ds(x2 + 3, 16), :]
        msg[pl.ds(X_NU2, 16), :] = HALF * nu_rows(ew, x2 + 3, T, ones_p, ones_m)
        msg[pl.ds(X_D1, 16), :] = ed[pl.ds(x1 + 3, 16), :]
        msg[pl.ds(X_D1 + 16, 6), :] = jnp.zeros((6, NZ), F32)


def fringe_table(fringe, table):
    total = T * lax.axis_size("gx")
    x = lax.broadcasted_iota(jnp.int32, (R, NZ), 0) - 1
    place = lax.axis_index("gx") * T + x - fringe[0]
    offset = lax.rem(place + 2 * total, jnp.full_like(place, total))
    width = fringe[1]
    phase = (math.pi * (offset.astype(F32) + 0.5)) / jnp.full((R, NZ), width, jnp.int32).astype(F32)
    sine = jnp.sin(phase)
    table[...] = jnp.where(offset < width, (DT * RATE) * (sine * sine), 0.0)


def rate_rows(table, x, rows):
    return jnp.broadcast_to(table[pl.ds(x + 1, 1), :], (rows, NZ))


def coefficients(nu, at, wind, lost, ones_p, ones_m):
    h = nu[pl.ds(at, R), :]
    hxp, hxm = nu[pl.ds(at + R, R), :], nu[pl.ds(at - R, R), :]
    hyp, hym = nu[pl.ds(at + 1, R), :], nu[pl.ds(at - 1, R), :]
    hzp, hzm = up_z(h) * ones_p, down_z(h) * ones_m
    pu, pv, pw = (HALF * v for v in wind)
    return (
        (1.0 - lost) - (6.0 * h + (hxp + hxm) + (hyp + hym) + (hzp + hzm)),
        h + hxp + pu,
        h + hxm - pu,
        h + hyp + pv,
        h + hym - pv,
        (h + hzp + pw) * ones_p,
        (h + hzm - pw) * ones_m,
    )


def stencil(a, at, rows, coefs, wind, ones_p, ones_m):
    c0, cxp, cxm, cyp, cym, czp, czm = coefs
    new, dx, dy, dz = [], [], [], []
    for c in range(4):
        mid = a[c, pl.ds(at, rows), :]
        xp, xm = a[c, pl.ds(at + R, rows), :], a[c, pl.ds(at - R, rows), :]
        yp, ym = a[c, pl.ds(at + 1, rows), :], a[c, pl.ds(at - 1, rows), :]
        zp, zm = up_z(mid), down_z(mid)
        if c < 3:
            new.append(c0 * mid + (cxp * xp + cxm * xm) + (cyp * yp + cym * ym) + (czp * zp + czm * zm))
        else:
            new.append(mid)
        dx.append(xp - xm if c in (0, 3) else None)
        dy.append(yp - ym if c in (1, 3) else None)
        dz.append(zp * ones_p - zm * ones_m if c in (2, 3) else None)
    sound = HALF * SOUND_SQ
    new[0] = new[0] + sound * dx[3]
    new[1] = new[1] + sound * dy[3]
    new[2] = new[2] + sound * dz[3]
    u, v, w = wind
    new[3] = new[3] + HALF * (u * dx[3] + v * dy[3] + w * dz[3] + dx[0] + dy[1] + dz[2])
    return new


def second_plane(own, at, cf_at, to, w, a1, cf, out, ones_p, ones_m):
    wind = [w[c, pl.ds(own, T), :] for c in range(3)]
    coefs = [cf[k, pl.ds(cf_at, T), :] for k in range(7)]
    new = stencil(a1, at, T, coefs, wind, ones_p, ones_m)
    for c in range(4):
        out[c, pl.ds(to, T), :] = new[c]


def inner(w, ew, ea, ed, main_a, fringe, nu, cf, a1, out, table):
    main = is_main()
    fringe_table(fringe, table)
    ones_p, ones_m = edges_z(R)

    def nu_plane(x, _):
        at = pl.multiple_of(x * R, 8)
        nu[pl.ds(at, R), :] = HALF * nu_rows(ew, at, R, ones_p, ones_m)
        return 0

    lax.fori_loop(1, T - 1, nu_plane, 0)

    def plane(x, _):
        at = pl.multiple_of(x * R, 8)
        wind = [ew[c, pl.ds(at, R), :] for c in range(3)]
        rate = rate_rows(table, x, R)
        coefs = coefficients(nu, at, wind, ed[pl.ds(at, R), :] + main * rate, ones_p, ones_m)
        new = stencil(ea, at, R, coefs, wind, ones_p, ones_m)
        push = (1.0 - main) * rate
        for c in range(4):
            a1[c, pl.ds(at, R), :] = new[c] if c == 3 else new[c] + push * main_a[c, pl.ds(at, R), :]
        for k in range(7):
            cf[k, pl.ds(at, R), :] = coefs[k]
        return 0

    lax.fori_loop(2, T - 2, plane, 0)
    short_p, short_m = edges_z(T)

    def later(x, _):
        own, at = pl.multiple_of(x * T, 8), x * R + 3
        second_plane(own, at, at, own, w, a1, cf, out, short_p, short_m)
        return 0

    lax.fori_loop(3, T - 3, later, 0)


def edges(first, second, ew, ea, ed, nu, main_a, table, cf_in, a1_in, cf, a1, sent, sw, sa, sd, sn):
    main = is_main()
    for group, shift in zip(KEPT, (LEFT, RIGHT)):
        for x in group:
            at, to = x * R, (x + shift) * R
            for c in range(3):
                sw[c, pl.ds(to, R), :] = ew[c, pl.ds(at, R), :]
            for c in range(4):
                sa[c, pl.ds(to, R), :] = ea[c, pl.ds(at, R), :]
            sd[pl.ds(to, R), :] = ed[pl.ds(at, R), :]
            sn[pl.ds(to, R), :] = nu[pl.ds(at, R), :]
    for msg, top in ((first, even("gx")), (second, jnp.logical_not(even("gx")))):
        p1, p2 = jnp.where(top, 8 * R, R), jnp.where(top, 9 * R, 0)
        for c in range(3):
            sw[c, pl.ds(p1 + 1, 20), :] = msg[pl.ds(X_U1 + 20 * c, 20), :]
            sw[c, pl.ds(p2 + 2, 18), :] = msg[pl.ds(X_U2 + 18 * c, 18), :]
        for c in range(4):
            sa[c, pl.ds(p1 + 2, 18), :] = msg[pl.ds(X_A1 + 18 * c, 18), :]
            sa[c, pl.ds(p2 + 3, 16), :] = msg[pl.ds(X_A2 + 16 * c, 16), :]
        sn[pl.ds(p2 + 3, 16), :] = msg[pl.ds(X_NU2, 16), :]
        sd[pl.ds(p1 + 3, 16), :] = msg[pl.ds(X_D1, 16), :]
    ones_p, ones_m = edges_z(R)

    def nu_plane(k, _):
        at = pl.multiple_of(jnp.where(k < 2, k + 1, k + 5) * R, 8)
        sn[pl.ds(at, R), :] = HALF * nu_rows(sw, at, R, ones_p, ones_m)
        return 0

    lax.fori_loop(0, 4, nu_plane, 0)

    def plane(k, _):
        p = jnp.where(k < 3, k + 1, k + 3)
        x = jnp.where(k < 3, k - 1, k + 11)
        at = pl.multiple_of(p * R, 8)
        to = pl.multiple_of(jnp.where(k < 3, k, k + 4) * R, 8)
        own = pl.multiple_of(jnp.clip(x, 0, T - 1) * R, 8)
        wind = [sw[c, pl.ds(at, R), :] for c in range(3)]
        rate = rate_rows(table, x, R)
        coefs = coefficients(sn, at, wind, sd[pl.ds(at, R), :] + main * rate, ones_p, ones_m)
        new = stencil(sa, at, R, coefs, wind, ones_p, ones_m)
        inside = jnp.logical_and(x >= 0, x < T).astype(F32)
        push = ((1.0 - main) * inside) * rate
        for c in range(4):
            a1[c, pl.ds(to, R), :] = new[c] if c == 3 else new[c] + push * main_a[c, pl.ds(own, R), :]
        keep = pl.multiple_of(jnp.where(k == 0, 6, jnp.where(k == 5, 7, jnp.where(k < 3, k - 1, k + 1))) * R, 8)
        for n in range(7):
            cf[n, pl.ds(keep, R), :] = coefs[n]
        return 0

    lax.fori_loop(0, 6, plane, 0)
    for x, p in ((2, 3), (3, 4), (12, 5), (13, 6)):
        for c in range(4):
            a1[c, pl.ds(p * R, R), :] = a1_in[c, pl.ds(x * R, R), :]
    for x, p in ((2, 2), (13, 3)):
        for n in range(7):
            cf[n, pl.ds(p * R, R), :] = cf_in[n, pl.ds(x * R, R), :]
    for c in range(3):
        sent[c, pl.ds(0, T), :] = sa[c, pl.ds(R + 3, T), :]
        for x in range(T):
            src = a1[c, pl.ds((x + 1 if x < 8 else x - 7) * R + 3, T), :] if x in (0, 1, 14, 15) else a1_in[
                c, pl.ds(x * R + 3, T), :
            ]
            sent[c, pl.ds((x + 1) * T, T), :] = src
        sent[c, pl.ds((T + 1) * T, T), :] = sa[c, pl.ds(8 * R + 3, T), :]


def second_edges(w, a1, cf, part):
    ones_p, ones_m = edges_z(T)

    def plane(k, _):
        x = jnp.where(k < 3, k, k + 10)
        p = jnp.where(k < 3, k + 1, k + 3)
        second_plane(pl.multiple_of(x * T, 8), p * R + 3, k * R + 3, pl.multiple_of(k * T, 8), w, a1, cf, part, ones_p, ones_m)
        return 0

    lax.fori_loop(0, 6, plane, 0)


def finish(part, part_edges, cf, main_a, table, out):
    other = 1.0 - is_main()
    for x in range(T):
        inside = 3 <= x < T - 3
        k = x if x < 8 else x - 10
        rate = rate_rows(table, x, T) * other
        src, at = (part, x * T) if inside else (part_edges, k * T)
        new = [src[c, pl.ds(at, T), :] for c in range(4)]
        for c in range(3):
            new[c] = new[c] + rate * main_a[c, pl.ds((x + 1) * T, T), :]
        if x in (0, T - 1):
            p, n, sign = (0, 2, -1.0) if x == 0 else (T + 1, 1, 1.0)
            rate = rate_rows(table, p - 1, T) * other
            beside = [rate * main_a[c, pl.ds(p * T, T), :] for c in range(3)]
            coef = cf[n, pl.ds(k * R + 3, T), :]
            for c in range(3):
                new[c] = new[c] + coef * beside[c]
            new[3] = new[3] + (sign * HALF) * beside[0]
        for c in range(4):
            out[c, pl.ds(x * T, T), :] = new[c]


def pairs(axis, offset):
    devices = lax.axis_size(axis)
    found = []
    for i in range(offset, devices + offset, 2):
        a, b = i % devices, (i + 1) % devices
        found += [(a, b), (b, a)]
    return found


def swap(first, second, axis):
    first = lax.ppermute(first, axis, pairs(axis, 0))
    second = lax.ppermute(second, axis, pairs(axis, 1))
    return first, second


def on_device(wind, adjoint, turbines, fringe_range):
    y_msg, x_msg = shape(Y_LEN, T, NZ), shape(X_LEN, NZ)
    tile = shape(4, T * T, NZ)
    y1, y2, w, a, t = call(
        pack_y,
        (y_msg, y_msg, shape(3, T * T, NZ), tile, jax.ShapeDtypeStruct((T * T, NZ), jnp.int32)),
        [HBM] * 3,
        scratch=[pltpu.SemaphoreType.DMA((3,))],
    )(
        *(
            pltpu.with_memory_space_constraint(v, pltpu.HBM)
            for v in (wind.reshape(3, T * T, NZ), adjoint.reshape(4, T * T, NZ), turbines.reshape(T * T, NZ))
        )
    )
    y1, y2 = swap(y1, y2, "gy")
    x1, x2 = call(
        pack_x,
        (x_msg, x_msg),
        [VMEM] * 5,
        scratch=[scratch(*planes(6, 3)), scratch(*planes(6, 4)), scratch(*planes(6))],
    )(w, a, t, y1, y2)
    x1, x2 = swap(x1, x2, "gx")
    ew, ea, ed, vel = call(
        spread_rows,
        (shape(*planes(T, 3)), shape(*planes(T, 4)), shape(*planes(T)), shape(3, T * R, NZ)),
        [VMEM] * 5,
        flops=10**6,
    )(w, a, t, y1, y2)
    main_a = lax.ppermute(vel, "dom", [(0, 1)])
    nu, cf, a1, part, table = call(
        inner,
        (shape(*planes(T)), shape(*planes(T, 7)), shape(*planes(T, 4)), tile, shape(R, NZ)),
        [VMEM] * 5 + [SMEM],
        flops=10**7,
    )(w, ew, ea, ed, main_a, fringe_range)
    cf_edges, a1_edges, sent = call(
        edges,
        (shape(*planes(8, 7)), shape(*planes(10, 4)), shape(3, (T + 2) * T, NZ)),
        [VMEM] * 10,
        scratch=[scratch(*planes(10, 3)), scratch(*planes(10, 4)), scratch(*planes(10)), scratch(*planes(10))],
    )(x1, x2, ew, ea, ed, nu, main_a, table, cf, a1)
    main_a1 = lax.ppermute(sent, "dom", [(0, 1)])
    part_edges = call(second_edges, shape(4, 6 * T, NZ), [VMEM] * 3, flops=10**6)(w, a1_edges, cf_edges)
    out = call(finish, tile, [VMEM] * 5)(part, part_edges, cf_edges, main_a1, table)
    return out.reshape(1, 4, T, T, NZ)


def solution(mesh):
    in_specs = (
        P("dom", None, "gx", "gy", None),
        P("dom", None, "gx", "gy", None),
        P("gx", "gy", None),
        P(),
    )
    out_specs = P("dom", None, "gx", "gy", None)
    return jax.shard_map(on_device, mesh=mesh, in_specs=in_specs, out_specs=out_specs, check_vma=False)
```

```python
import math

import jax
import jax.numpy as jnp
from jax import lax
from jax.experimental import pallas as pl
from jax.experimental.pallas import tpu as pltpu
from jax.sharding import PartitionSpec as P


DT = 0.1
HALF = 0.5 * DT
SMAG = 0.1
SOUND_SQ = 4.0
DRAG = 1.0
RATE = 3.0

T = 16
NZ = 128
R = 24
SPARE = 8
F32 = jnp.float32
VMEM = pl.BlockSpec(memory_space=pltpu.VMEM)
SMEM = pl.BlockSpec(memory_space=pltpu.SMEM)
HBM = pl.BlockSpec(memory_space=pltpu.HBM)

Y_WIND, Y_ADJ, Y_DRAG, Y_LEN = 0, 9, 17, 18
X_U1, X_U2, X_A1, X_A2, X_NU2, X_D1, X_LEN = 0, 60, 114, 186, 250, 266, 288
LEFT, RIGHT = 2, -8
KEPT = ((0, 1, 2), (13, 14, 15))


def shape(*dims):
    return jax.ShapeDtypeStruct(dims, F32)


def planes(n, *lead):
    return lead + (n * R + SPARE, NZ)


def call(body, outs, specs, scratch=(), flops=0):
    made = pl.pallas_call(
        body,
        out_shape=outs,
        in_specs=specs,
        out_specs=jax.tree.map(lambda _: VMEM, outs),
        scratch_shapes=scratch,
        compiler_params=pltpu.CompilerParams(vmem_limit_bytes=16 * 1024 * 1024),
        cost_estimate=pl.CostEstimate(flops=flops, bytes_accessed=0, transcendentals=0),
    )
    return made


def scratch(*dims):
    return pltpu.VMEM(dims, F32)


def is_main():
    return (lax.axis_index("dom") == 0).astype(F32)


def sends_up():
    return True, False


def from_above():
    return False, True


def up_z(v):
    return pltpu.roll(v, NZ - 1, 1)


def down_z(v):
    return pltpu.roll(v, 1, 1)


def edges_z(rows):
    lane = lax.broadcasted_iota(jnp.int32, (rows, NZ), 1)
    return (lane < NZ - 1).astype(F32), (lane > 0).astype(F32)


def drag_rows(u, v, w, turb):
    return (DT * DRAG) * turb * jnp.sqrt(u * u + v * v + w * w) * is_main()


def pack_y(w_hbm, a_hbm, t_hbm, first, second, w, a, t, sems):
    copies = [
        pltpu.make_async_copy(src, dst, sems.at[k])
        for k, (src, dst) in enumerate(((w_hbm, w), (a_hbm, a), (t_hbm, t)))
    ]
    for copy in copies:
        copy.start()
    sides = []
    for msg, top in zip((first, second), sends_up()):
        sides.append((msg, jnp.where(top, T - 3, 0), jnp.where(top, T - 2, 0), jnp.where(top, T - 1, 0)))
    copies[0].wait()
    for msg, edge, _, _ in sides:
        for c in range(3):
            for l in range(3):
                msg[Y_WIND + 3 * c + l] = w[c, pl.ds(edge + l, T, stride=T), :]
    copies[1].wait()
    for msg, _, edge, _ in sides:
        for c in range(4):
            for l in range(2):
                msg[Y_ADJ + 2 * c + l] = a[c, pl.ds(edge + l, T, stride=T), :]
    copies[2].wait()
    for msg, _, _, near in sides:
        u, v, z = (w[c, pl.ds(near, T, stride=T), :] for c in range(3))
        turb = t[pl.ds(near, T, stride=T), :].astype(F32)
        msg[Y_DRAG] = drag_rows(u, v, z, turb)


def y_rims(first, second, ew, ea, ed, shift, firsts, count):
    for msg, top in zip((first, second), from_above()):
        base = (firsts + shift) * R
        at_w, at_a, at_d = (base + jnp.where(top, T + 3, k) for k in range(3))
        own = pl.ds(firsts, count)
        for c in range(3):
            for l in range(3):
                ew[c, pl.ds(at_w + l, count, stride=R), :] = msg[Y_WIND + 3 * c + l, own]
        for c in range(4):
            for l in range(2):
                ea[c, pl.ds(at_a + l, count, stride=R), :] = msg[Y_ADJ + 2 * c + l, own]
        ed[pl.ds(at_d, count, stride=R), :] = msg[Y_DRAG, own]


def own_rows(x, to, w, a, t, ew, ea, ed):
    wind = [w[c, pl.ds(x * T, T), :] for c in range(3)]
    for c in range(3):
        ew[c, pl.ds(to * R + 3, T), :] = wind[c]
    for c in range(4):
        ea[c, pl.ds(to * R + 3, T), :] = a[c, pl.ds(x * T, T), :]
    ed[pl.ds(to * R + 3, T), :] = drag_rows(*wind, t[pl.ds(x * T, T), :].astype(F32))


def spread_rows(w, a, t, first, second, ew, ea, ed, vel):
    for x in range(T):
        own_rows(x, x, w, a, t, ew, ea, ed)
    y_rims(first, second, ew, ea, ed, 0, 0, T)
    vel[...] = ea[pl.ds(0, 3), pl.ds(0, T * R), :]


def nu_rows(ew, at, rows, ones_p, ones_m):
    g = []
    for c in range(3):
        mid = ew[c, pl.ds(at, rows), :]
        gx = ew[c, pl.ds(at + R, rows), :] - ew[c, pl.ds(at - R, rows), :]
        gy = ew[c, pl.ds(at + 1, rows), :] - ew[c, pl.ds(at - 1, rows), :]
        gz = up_z(mid) * ones_p - down_z(mid) * ones_m
        g.append((gx, gy, gz))
    diag = g[0][0] * g[0][0] + g[1][1] * g[1][1] + g[2][2] * g[2][2]
    xy = g[1][0] + g[0][1]
    xz = g[2][0] + g[0][2]
    yz = g[2][1] + g[1][2]
    return SMAG * jnp.sqrt(0.5 * diag + 0.25 * (xy * xy + xz * xz + yz * yz))


def pack_x(w, a, t, first_y, second_y, first, second, ew, ea, ed):
    for x in KEPT[0] + KEPT[1]:
        own_rows(x, x if x < 8 else x - 10, w, a, t, ew, ea, ed)
    y_rims(first_y, second_y, ew, ea, ed, 0, 0, 3)
    y_rims(first_y, second_y, ew, ea, ed, -10, 13, 3)
    ones_p, ones_m = edges_z(T)
    for msg, top in zip((first, second), sends_up()):
        x1, x2 = jnp.where(top, 5 * R, 0), jnp.where(top, 4 * R, R)
        for c in range(3):
            msg[pl.ds(X_U1 + 20 * c, 20), :] = ew[c, pl.ds(x1 + 1, 20), :]
            msg[pl.ds(X_U2 + 18 * c, 18), :] = ew[c, pl.ds(x2 + 2, 18), :]
        for c in range(4):
            msg[pl.ds(X_A1 + 18 * c, 18), :] = ea[c, pl.ds(x1 + 2, 18), :]
            msg[pl.ds(X_A2 + 16 * c, 16), :] = ea[c, pl.ds(x2 + 3, 16), :]
        msg[pl.ds(X_NU2, 16), :] = HALF * nu_rows(ew, x2 + 3, T, ones_p, ones_m)
        msg[pl.ds(X_D1, 16), :] = ed[pl.ds(x1 + 3, 16), :]
        msg[pl.ds(X_D1 + 16, 6), :] = jnp.zeros((6, NZ), F32)


def fringe_table(fringe, table):
    total = T * lax.axis_size("gx")
    x = lax.broadcasted_iota(jnp.int32, (R, NZ), 0) - 1
    place = lax.axis_index("gx") * T + x - fringe[0]
    offset = lax.rem(place + 2 * total, jnp.full_like(place, total))
    width = fringe[1]
    phase = (math.pi * (offset.astype(F32) + 0.5)) / jnp.full((R, NZ), width, jnp.int32).astype(F32)
    sine = jnp.sin(phase)
    table[...] = jnp.where(offset < width, (DT * RATE) * (sine * sine), 0.0)


def rate_rows(table, x, rows):
    return jnp.broadcast_to(table[pl.ds(x + 1, 1), :], (rows, NZ))


def coefficients(nu, at, wind, lost, ones_p, ones_m):
    h = nu[pl.ds(at, R), :]
    hxp, hxm = nu[pl.ds(at + R, R), :], nu[pl.ds(at - R, R), :]
    hyp, hym = nu[pl.ds(at + 1, R), :], nu[pl.ds(at - 1, R), :]
    hzp, hzm = up_z(h) * ones_p, down_z(h) * ones_m
    pu, pv, pw = (HALF * v for v in wind)
    return (
        (1.0 - lost) - (6.0 * h + (hxp + hxm) + (hyp + hym) + (hzp + hzm)),
        h + hxp + pu,
        h + hxm - pu,
        h + hyp + pv,
        h + hym - pv,
        (h + hzp + pw) * ones_p,
        (h + hzm - pw) * ones_m,
    )


def stencil(a, at, rows, coefs, wind, ones_p, ones_m):
    c0, cxp, cxm, cyp, cym, czp, czm = coefs
    new, dx, dy, dz = [], [], [], []
    for c in range(4):
        mid = a[c, pl.ds(at, rows), :]
        xp, xm = a[c, pl.ds(at + R, rows), :], a[c, pl.ds(at - R, rows), :]
        yp, ym = a[c, pl.ds(at + 1, rows), :], a[c, pl.ds(at - 1, rows), :]
        zp, zm = up_z(mid), down_z(mid)
        if c < 3:
            new.append(c0 * mid + (cxp * xp + cxm * xm) + (cyp * yp + cym * ym) + (czp * zp + czm * zm))
        else:
            new.append(mid)
        dx.append(xp - xm if c in (0, 3) else None)
        dy.append(yp - ym if c in (1, 3) else None)
        dz.append(zp * ones_p - zm * ones_m if c in (2, 3) else None)
    sound = HALF * SOUND_SQ
    new[0] = new[0] + sound * dx[3]
    new[1] = new[1] + sound * dy[3]
    new[2] = new[2] + sound * dz[3]
    u, v, w = wind
    new[3] = new[3] + HALF * (u * dx[3] + v * dy[3] + w * dz[3] + dx[0] + dy[1] + dz[2])
    return new


def second_plane(own, at, cf_at, to, w, a1, cf, out, ones_p, ones_m):
    wind = [w[c, pl.ds(own, T), :] for c in range(3)]
    coefs = [cf[k, pl.ds(cf_at, T), :] for k in range(7)]
    new = stencil(a1, at, T, coefs, wind, ones_p, ones_m)
    for c in range(4):
        out[c, pl.ds(to, T), :] = new[c]


def inner(w, ew, ea, ed, main_a, fringe, nu, cf, a1, out, table):
    main = is_main()
    fringe_table(fringe, table)
    ones_p, ones_m = edges_z(R)

    def nu_plane(x, _):
        at = pl.multiple_of(x * R, 8)
        nu[pl.ds(at, R), :] = HALF * nu_rows(ew, at, R, ones_p, ones_m)
        return 0

    lax.fori_loop(1, T - 1, nu_plane, 0)

    def plane(x, _):
        at = pl.multiple_of(x * R, 8)
        wind = [ew[c, pl.ds(at, R), :] for c in range(3)]
        rate = rate_rows(table, x, R)
        coefs = coefficients(nu, at, wind, ed[pl.ds(at, R), :] + main * rate, ones_p, ones_m)
        new = stencil(ea, at, R, coefs, wind, ones_p, ones_m)
        push = (1.0 - main) * rate
        for c in range(4):
            a1[c, pl.ds(at, R), :] = new[c] if c == 3 else new[c] + push * main_a[c, pl.ds(at, R), :]
        for k in range(7):
            cf[k, pl.ds(at, R), :] = coefs[k]
        return 0

    lax.fori_loop(2, T - 2, plane, 0)
    short_p, short_m = edges_z(T)

    def later(x, _):
        own, at = pl.multiple_of(x * T, 8), x * R + 3
        second_plane(own, at, at, own, w, a1, cf, out, short_p, short_m)
        return 0

    lax.fori_loop(3, T - 3, later, 0)


def edges(first, second, ew, ea, ed, nu, main_a, table, cf_in, a1_in, cf, a1, sent, sw, sa, sd, sn):
    main = is_main()
    for group, shift in zip(KEPT, (LEFT, RIGHT)):
        for x in group:
            at, to = x * R, (x + shift) * R
            for c in range(3):
                sw[c, pl.ds(to, R), :] = ew[c, pl.ds(at, R), :]
            for c in range(4):
                sa[c, pl.ds(to, R), :] = ea[c, pl.ds(at, R), :]
            sd[pl.ds(to, R), :] = ed[pl.ds(at, R), :]
            sn[pl.ds(to, R), :] = nu[pl.ds(at, R), :]
    for msg, top in zip((first, second), from_above()):
        p1, p2 = jnp.where(top, 8 * R, R), jnp.where(top, 9 * R, 0)
        for c in range(3):
            sw[c, pl.ds(p1 + 1, 20), :] = msg[pl.ds(X_U1 + 20 * c, 20), :]
            sw[c, pl.ds(p2 + 2, 18), :] = msg[pl.ds(X_U2 + 18 * c, 18), :]
        for c in range(4):
            sa[c, pl.ds(p1 + 2, 18), :] = msg[pl.ds(X_A1 + 18 * c, 18), :]
            sa[c, pl.ds(p2 + 3, 16), :] = msg[pl.ds(X_A2 + 16 * c, 16), :]
        sn[pl.ds(p2 + 3, 16), :] = msg[pl.ds(X_NU2, 16), :]
        sd[pl.ds(p1 + 3, 16), :] = msg[pl.ds(X_D1, 16), :]
    ones_p, ones_m = edges_z(R)

    def nu_plane(k, _):
        at = pl.multiple_of(jnp.where(k < 2, k + 1, k + 5) * R, 8)
        sn[pl.ds(at, R), :] = HALF * nu_rows(sw, at, R, ones_p, ones_m)
        return 0

    lax.fori_loop(0, 4, nu_plane, 0)

    def plane(k, _):
        p = jnp.where(k < 3, k + 1, k + 3)
        x = jnp.where(k < 3, k - 1, k + 11)
        at = pl.multiple_of(p * R, 8)
        to = pl.multiple_of(jnp.where(k < 3, k, k + 4) * R, 8)
        own = pl.multiple_of(jnp.clip(x, 0, T - 1) * R, 8)
        wind = [sw[c, pl.ds(at, R), :] for c in range(3)]
        rate = rate_rows(table, x, R)
        coefs = coefficients(sn, at, wind, sd[pl.ds(at, R), :] + main * rate, ones_p, ones_m)
        new = stencil(sa, at, R, coefs, wind, ones_p, ones_m)
        inside = jnp.logical_and(x >= 0, x < T).astype(F32)
        push = ((1.0 - main) * inside) * rate
        for c in range(4):
            a1[c, pl.ds(to, R), :] = new[c] if c == 3 else new[c] + push * main_a[c, pl.ds(own, R), :]
        keep = pl.multiple_of(jnp.where(k == 0, 6, jnp.where(k == 5, 7, jnp.where(k < 3, k - 1, k + 1))) * R, 8)
        for n in range(7):
            cf[n, pl.ds(keep, R), :] = coefs[n]
        return 0

    lax.fori_loop(0, 6, plane, 0)
    for x, p in ((2, 3), (3, 4), (12, 5), (13, 6)):
        for c in range(4):
            a1[c, pl.ds(p * R, R), :] = a1_in[c, pl.ds(x * R, R), :]
    for x, p in ((2, 2), (13, 3)):
        for n in range(7):
            cf[n, pl.ds(p * R, R), :] = cf_in[n, pl.ds(x * R, R), :]
    for c in range(3):
        sent[c, pl.ds(0, T), :] = sa[c, pl.ds(R + 3, T), :]
        for x in range(T):
            src = a1[c, pl.ds((x + 1 if x < 8 else x - 7) * R + 3, T), :] if x in (0, 1, 14, 15) else a1_in[
                c, pl.ds(x * R + 3, T), :
            ]
            sent[c, pl.ds((x + 1) * T, T), :] = src
        sent[c, pl.ds((T + 1) * T, T), :] = sa[c, pl.ds(8 * R + 3, T), :]


def second_edges(w, a1, cf, part):
    ones_p, ones_m = edges_z(T)

    def plane(k, _):
        x = jnp.where(k < 3, k, k + 10)
        p = jnp.where(k < 3, k + 1, k + 3)
        second_plane(pl.multiple_of(x * T, 8), p * R + 3, k * R + 3, pl.multiple_of(k * T, 8), w, a1, cf, part, ones_p, ones_m)
        return 0

    lax.fori_loop(0, 6, plane, 0)


def finish(part, part_edges, cf, main_a, table, out):
    other = 1.0 - is_main()
    for x in range(T):
        inside = 3 <= x < T - 3
        k = x if x < 8 else x - 10
        rate = rate_rows(table, x, T) * other
        src, at = (part, x * T) if inside else (part_edges, k * T)
        new = [src[c, pl.ds(at, T), :] for c in range(4)]
        for c in range(3):
            new[c] = new[c] + rate * main_a[c, pl.ds((x + 1) * T, T), :]
        if x in (0, T - 1):
            p, n, sign = (0, 2, -1.0) if x == 0 else (T + 1, 1, 1.0)
            rate = rate_rows(table, p - 1, T) * other
            beside = [rate * main_a[c, pl.ds(p * T, T), :] for c in range(3)]
            coef = cf[n, pl.ds(k * R + 3, T), :]
            for c in range(3):
                new[c] = new[c] + coef * beside[c]
            new[3] = new[3] + (sign * HALF) * beside[0]
        for c in range(4):
            out[c, pl.ds(x * T, T), :] = new[c]


def ring(axis, by):
    devices = lax.axis_size(axis)
    return [(i, (i + by) % devices) for i in range(devices)]


def exchange(first, second, axis):
    first = lax.ppermute(first, axis, ring(axis, 1))
    second = lax.ppermute(second, axis, ring(axis, -1))
    return first, second


def on_device(wind, adjoint, turbines, fringe_range):
    y_msg, x_msg = shape(Y_LEN, T, NZ), shape(X_LEN, NZ)
    tile = shape(4, T * T, NZ)
    y1, y2, w, a, t = call(
        pack_y,
        (y_msg, y_msg, shape(3, T * T, NZ), tile, jax.ShapeDtypeStruct((T * T, NZ), jnp.int32)),
        [HBM] * 3,
        scratch=[pltpu.SemaphoreType.DMA((3,))],
    )(
        *(
            pltpu.with_memory_space_constraint(v, pltpu.HBM)
            for v in (wind.reshape(3, T * T, NZ), adjoint.reshape(4, T * T, NZ), turbines.reshape(T * T, NZ))
        )
    )
    y1, y2 = exchange(y1, y2, "gy")
    x1, x2 = call(
        pack_x,
        (x_msg, x_msg),
        [VMEM] * 5,
        scratch=[scratch(*planes(6, 3)), scratch(*planes(6, 4)), scratch(*planes(6))],
    )(w, a, t, y1, y2)
    x1, x2 = exchange(x1, x2, "gx")
    ew, ea, ed, vel = call(
        spread_rows,
        (shape(*planes(T, 3)), shape(*planes(T, 4)), shape(*planes(T)), shape(3, T * R, NZ)),
        [VMEM] * 5,
        flops=10**6,
    )(w, a, t, y1, y2)
    main_a = lax.ppermute(vel, "dom", [(0, 1)])
    nu, cf, a1, part, table = call(
        inner,
        (shape(*planes(T)), shape(*planes(T, 7)), shape(*planes(T, 4)), tile, shape(R, NZ)),
        [VMEM] * 5 + [SMEM],
        flops=10**7,
    )(w, ew, ea, ed, main_a, fringe_range)
    cf_edges, a1_edges, sent = call(
        edges,
        (shape(*planes(8, 7)), shape(*planes(10, 4)), shape(3, (T + 2) * T, NZ)),
        [VMEM] * 10,
        scratch=[scratch(*planes(10, 3)), scratch(*planes(10, 4)), scratch(*planes(10)), scratch(*planes(10))],
    )(x1, x2, ew, ea, ed, nu, main_a, table, cf, a1)
    main_a1 = lax.ppermute(sent, "dom", [(0, 1)])
    part_edges = call(second_edges, shape(4, 6 * T, NZ), [VMEM] * 3, flops=10**6)(w, a1_edges, cf_edges)
    out = call(finish, tile, [VMEM] * 5)(part, part_edges, cf_edges, main_a1, table)
    return out.reshape(1, 4, T, T, NZ)


def solution(mesh):
    in_specs = (
        P("dom", None, "gx", "gy", None),
        P("dom", None, "gx", "gy", None),
        P("gx", "gy", None),
        P(),
    )
    out_specs = P("dom", None, "gx", "gy", None)
    return jax.shard_map(on_device, mesh=mesh, in_specs=in_specs, out_specs=out_specs, check_vma=False)
```

```python
import math

import jax
import jax.numpy as jnp
from jax import lax
from jax.experimental import pallas as pl
from jax.experimental.pallas import tpu as pltpu
from jax.sharding import PartitionSpec as P


DT = 0.1
HALF = 0.5 * DT
SMAG = 0.1
SOUND_SQ = 4.0
DRAG = 1.0
RATE = 3.0

T = 16
NZ = 128
R = 24
SPARE = 8
F32 = jnp.float32
VMEM = pl.BlockSpec(memory_space=pltpu.VMEM)
SMEM = pl.BlockSpec(memory_space=pltpu.SMEM)
HBM = pl.BlockSpec(memory_space=pltpu.HBM)

Y_WIND, Y_ADJ, Y_DRAG, Y_LEN = 0, 9, 17, 18
X_U1, X_U2, X_A1, X_A2, X_NU2, X_D1, X_LEN = 0, 60, 114, 186, 250, 266, 288
LEFT, RIGHT = 2, -8
KEPT = ((0, 1, 2), (13, 14, 15))


def shape(*dims):
    return jax.ShapeDtypeStruct(dims, F32)


def planes(n, *lead):
    return lead + (n * R + SPARE, NZ)


def call(body, outs, specs, scratch=(), flops=0):
    made = pl.pallas_call(
        body,
        out_shape=outs,
        in_specs=specs,
        out_specs=jax.tree.map(lambda _: VMEM, outs),
        scratch_shapes=scratch,
        compiler_params=pltpu.CompilerParams(vmem_limit_bytes=16 * 1024 * 1024),
        cost_estimate=pl.CostEstimate(flops=flops, bytes_accessed=0, transcendentals=0),
    )
    return made


def scratch(*dims):
    return pltpu.VMEM(dims, F32)


def is_main():
    return (lax.axis_index("dom") == 0).astype(F32)


def sends_up():
    return True, False


def from_above():
    return False, True


def up_z(v):
    return pltpu.roll(v, NZ - 1, 1)


def down_z(v):
    return pltpu.roll(v, 1, 1)


def edges_z(rows):
    lane = lax.broadcasted_iota(jnp.int32, (rows, NZ), 1)
    return (lane < NZ - 1).astype(F32), (lane > 0).astype(F32)


def drag_rows(u, v, w, turb):
    return (DT * DRAG) * turb * jnp.sqrt(u * u + v * v + w * w) * is_main()


def pack_y(w_hbm, a_hbm, t_hbm, first, second, w, a, t, sems):
    copies = [
        pltpu.make_async_copy(src, dst, sems.at[k])
        for k, (src, dst) in enumerate(((w_hbm, w), (a_hbm, a), (t_hbm, t)))
    ]
    for copy in copies:
        copy.start()
    sides = []
    for msg, top in zip((first, second), sends_up()):
        sides.append((msg, jnp.where(top, T - 3, 0), jnp.where(top, T - 2, 0), jnp.where(top, T - 1, 0)))
    copies[0].wait()
    for msg, edge, _, _ in sides:
        for c in range(3):
            for l in range(3):
                msg[Y_WIND + 3 * c + l] = w[c, pl.ds(edge + l, T, stride=T), :]
    copies[1].wait()
    for msg, _, edge, _ in sides:
        for c in range(4):
            for l in range(2):
                msg[Y_ADJ + 2 * c + l] = a[c, pl.ds(edge + l, T, stride=T), :]
    copies[2].wait()
    for msg, _, _, near in sides:
        u, v, z = (w[c, pl.ds(near, T, stride=T), :] for c in range(3))
        turb = t[pl.ds(near, T, stride=T), :].astype(F32)
        msg[Y_DRAG] = drag_rows(u, v, z, turb)


def y_rims(first, second, ew, ea, ed, shift, firsts, count):
    for msg, top in zip((first, second), from_above()):
        base = (firsts + shift) * R
        at_w, at_a, at_d = (base + jnp.where(top, T + 3, k) for k in range(3))
        own = pl.ds(firsts, count)
        for c in range(3):
            for l in range(3):
                ew[c, pl.ds(at_w + l, count, stride=R), :] = msg[Y_WIND + 3 * c + l, own]
        for c in range(4):
            for l in range(2):
                ea[c, pl.ds(at_a + l, count, stride=R), :] = msg[Y_ADJ + 2 * c + l, own]
        ed[pl.ds(at_d, count, stride=R), :] = msg[Y_DRAG, own]


def own_rows(x, to, w, a, t, ew, ea, ed):
    wind = [w[c, pl.ds(x * T, T), :] for c in range(3)]
    for c in range(3):
        ew[c, pl.ds(to * R + 3, T), :] = wind[c]
    for c in range(4):
        ea[c, pl.ds(to * R + 3, T), :] = a[c, pl.ds(x * T, T), :]
    ed[pl.ds(to * R + 3, T), :] = drag_rows(*wind, t[pl.ds(x * T, T), :].astype(F32))


def spread_rows(w, a, t, first, second, main_a, ew, ea, ed, vel):
    for x in range(T):
        own_rows(x, x, w, a, t, ew, ea, ed)
        for c in range(3):
            vel[c, pl.ds(x * R, R), :] = jnp.zeros((R, NZ), F32)
            vel[c, pl.ds(x * R + 3, T), :] = main_a[c, pl.ds(x * T, T), :]
    y_rims(first, second, ew, ea, ed, 0, 0, T)


def nu_rows(ew, at, rows, ones_p, ones_m):
    g = []
    for c in range(3):
        mid = ew[c, pl.ds(at, rows), :]
        gx = ew[c, pl.ds(at + R, rows), :] - ew[c, pl.ds(at - R, rows), :]
        gy = ew[c, pl.ds(at + 1, rows), :] - ew[c, pl.ds(at - 1, rows), :]
        gz = up_z(mid) * ones_p - down_z(mid) * ones_m
        g.append((gx, gy, gz))
    diag = g[0][0] * g[0][0] + g[1][1] * g[1][1] + g[2][2] * g[2][2]
    xy = g[1][0] + g[0][1]
    xz = g[2][0] + g[0][2]
    yz = g[2][1] + g[1][2]
    return SMAG * jnp.sqrt(0.5 * diag + 0.25 * (xy * xy + xz * xz + yz * yz))


def pack_x(w, a, t, first_y, second_y, first, second, ew, ea, ed):
    for x in KEPT[0] + KEPT[1]:
        own_rows(x, x if x < 8 else x - 10, w, a, t, ew, ea, ed)
    y_rims(first_y, second_y, ew, ea, ed, 0, 0, 3)
    y_rims(first_y, second_y, ew, ea, ed, -10, 13, 3)
    ones_p, ones_m = edges_z(T)
    for msg, top in zip((first, second), sends_up()):
        x1, x2 = jnp.where(top, 5 * R, 0), jnp.where(top, 4 * R, R)
        for c in range(3):
            msg[pl.ds(X_U1 + 20 * c, 20), :] = ew[c, pl.ds(x1 + 1, 20), :]
            msg[pl.ds(X_U2 + 18 * c, 18), :] = ew[c, pl.ds(x2 + 2, 18), :]
        for c in range(4):
            msg[pl.ds(X_A1 + 18 * c, 18), :] = ea[c, pl.ds(x1 + 2, 18), :]
            msg[pl.ds(X_A2 + 16 * c, 16), :] = ea[c, pl.ds(x2 + 3, 16), :]
        msg[pl.ds(X_NU2, 16), :] = HALF * nu_rows(ew, x2 + 3, T, ones_p, ones_m)
        msg[pl.ds(X_D1, 16), :] = ed[pl.ds(x1 + 3, 16), :]
        msg[pl.ds(X_D1 + 16, 6), :] = jnp.zeros((6, NZ), F32)


def fringe_table(fringe, table):
    total = T * lax.axis_size("gx")
    x = lax.broadcasted_iota(jnp.int32, (R, NZ), 0) - 1
    place = lax.axis_index("gx") * T + x - fringe[0]
    offset = lax.rem(place + 2 * total, jnp.full_like(place, total))
    width = fringe[1]
    phase = (math.pi * (offset.astype(F32) + 0.5)) / jnp.full((R, NZ), width, jnp.int32).astype(F32)
    sine = jnp.sin(phase)
    table[...] = jnp.where(offset < width, (DT * RATE) * (sine * sine), 0.0)


def rate_rows(table, x, rows):
    return jnp.broadcast_to(table[pl.ds(x + 1, 1), :], (rows, NZ))


def coefficients(nu, at, wind, lost, ones_p, ones_m):
    h = nu[pl.ds(at, R), :]
    hxp, hxm = nu[pl.ds(at + R, R), :], nu[pl.ds(at - R, R), :]
    hyp, hym = nu[pl.ds(at + 1, R), :], nu[pl.ds(at - 1, R), :]
    hzp, hzm = up_z(h) * ones_p, down_z(h) * ones_m
    pu, pv, pw = (HALF * v for v in wind)
    return (
        (1.0 - lost) - (6.0 * h + (hxp + hxm) + (hyp + hym) + (hzp + hzm)),
        h + hxp + pu,
        h + hxm - pu,
        h + hyp + pv,
        h + hym - pv,
        (h + hzp + pw) * ones_p,
        (h + hzm - pw) * ones_m,
    )


def stencil(a, at, rows, coefs, wind, ones_p, ones_m):
    c0, cxp, cxm, cyp, cym, czp, czm = coefs
    new, dx, dy, dz = [], [], [], []
    for c in range(4):
        mid = a[c, pl.ds(at, rows), :]
        xp, xm = a[c, pl.ds(at + R, rows), :], a[c, pl.ds(at - R, rows), :]
        yp, ym = a[c, pl.ds(at + 1, rows), :], a[c, pl.ds(at - 1, rows), :]
        zp, zm = up_z(mid), down_z(mid)
        if c < 3:
            new.append(c0 * mid + (cxp * xp + cxm * xm) + (cyp * yp + cym * ym) + (czp * zp + czm * zm))
        else:
            new.append(mid)
        dx.append(xp - xm if c in (0, 3) else None)
        dy.append(yp - ym if c in (1, 3) else None)
        dz.append(zp * ones_p - zm * ones_m if c in (2, 3) else None)
    sound = HALF * SOUND_SQ
    new[0] = new[0] + sound * dx[3]
    new[1] = new[1] + sound * dy[3]
    new[2] = new[2] + sound * dz[3]
    u, v, w = wind
    new[3] = new[3] + HALF * (u * dx[3] + v * dy[3] + w * dz[3] + dx[0] + dy[1] + dz[2])
    return new


def second_plane(own, at, cf_at, to, w, a1, cf, out, ones_p, ones_m):
    wind = [w[c, pl.ds(own, T), :] for c in range(3)]
    coefs = [cf[k, pl.ds(cf_at, T), :] for k in range(7)]
    new = stencil(a1, at, T, coefs, wind, ones_p, ones_m)
    for c in range(4):
        out[c, pl.ds(to, T), :] = new[c]


def inner(w, ew, ea, ed, main_a, fringe, nu, cf, a1, out, table, inside):
    main = is_main()
    fringe_table(fringe, table)
    ones_p, ones_m = edges_z(R)

    def nu_plane(x, _):
        at = pl.multiple_of(x * R, 8)
        nu[pl.ds(at, R), :] = HALF * nu_rows(ew, at, R, ones_p, ones_m)
        return 0

    lax.fori_loop(1, T - 1, nu_plane, 0)

    def plane(x, _):
        at = pl.multiple_of(x * R, 8)
        wind = [ew[c, pl.ds(at, R), :] for c in range(3)]
        rate = rate_rows(table, x, R)
        coefs = coefficients(nu, at, wind, ed[pl.ds(at, R), :] + main * rate, ones_p, ones_m)
        new = stencil(ea, at, R, coefs, wind, ones_p, ones_m)
        push = (1.0 - main) * rate
        for c in range(4):
            a1[c, pl.ds(at, R), :] = new[c] if c == 3 else new[c] + push * main_a[c, pl.ds(at, R), :]
        for k in range(7):
            cf[k, pl.ds(at, R), :] = coefs[k]
        return 0

    lax.fori_loop(2, T - 2, plane, 0)
    for c in range(3):
        for x in range(2, T - 2):
            inside[c, pl.ds((x - 2) * T, T), :] = a1[c, pl.ds(x * R + 3, T), :]
    short_p, short_m = edges_z(T)

    def later(x, _):
        own, at = pl.multiple_of(x * T, 8), x * R + 3
        second_plane(own, at, at, own, w, a1, cf, out, short_p, short_m)
        return 0

    lax.fori_loop(3, T - 3, later, 0)


def edges(first, second, ew, ea, ed, nu, main_a, table, cf_in, a1_in, cf, a1, sent, beside, sw, sa, sd, sn):
    main = is_main()
    for group, shift in zip(KEPT, (LEFT, RIGHT)):
        for x in group:
            at, to = x * R, (x + shift) * R
            for c in range(3):
                sw[c, pl.ds(to, R), :] = ew[c, pl.ds(at, R), :]
            for c in range(4):
                sa[c, pl.ds(to, R), :] = ea[c, pl.ds(at, R), :]
            sd[pl.ds(to, R), :] = ed[pl.ds(at, R), :]
            sn[pl.ds(to, R), :] = nu[pl.ds(at, R), :]
    for msg, top in zip((first, second), from_above()):
        p1, p2 = jnp.where(top, 8 * R, R), jnp.where(top, 9 * R, 0)
        for c in range(3):
            sw[c, pl.ds(p1 + 1, 20), :] = msg[pl.ds(X_U1 + 20 * c, 20), :]
            sw[c, pl.ds(p2 + 2, 18), :] = msg[pl.ds(X_U2 + 18 * c, 18), :]
        for c in range(4):
            sa[c, pl.ds(p1 + 2, 18), :] = msg[pl.ds(X_A1 + 18 * c, 18), :]
            sa[c, pl.ds(p2 + 3, 16), :] = msg[pl.ds(X_A2 + 16 * c, 16), :]
        sn[pl.ds(p2 + 3, 16), :] = msg[pl.ds(X_NU2, 16), :]
        sd[pl.ds(p1 + 3, 16), :] = msg[pl.ds(X_D1, 16), :]
    ones_p, ones_m = edges_z(R)

    def nu_plane(k, _):
        at = pl.multiple_of(jnp.where(k < 2, k + 1, k + 5) * R, 8)
        sn[pl.ds(at, R), :] = HALF * nu_rows(sw, at, R, ones_p, ones_m)
        return 0

    lax.fori_loop(0, 4, nu_plane, 0)

    def plane(k, _):
        p = jnp.where(k < 3, k + 1, k + 3)
        x = jnp.where(k < 3, k - 1, k + 11)
        at = pl.multiple_of(p * R, 8)
        to = pl.multiple_of(jnp.where(k < 3, k, k + 4) * R, 8)
        own = pl.multiple_of(jnp.clip(x, 0, T - 1) * R, 8)
        wind = [sw[c, pl.ds(at, R), :] for c in range(3)]
        rate = rate_rows(table, x, R)
        coefs = coefficients(sn, at, wind, sd[pl.ds(at, R), :] + main * rate, ones_p, ones_m)
        new = stencil(sa, at, R, coefs, wind, ones_p, ones_m)
        inside = jnp.logical_and(x >= 0, x < T).astype(F32)
        push = ((1.0 - main) * inside) * rate
        for c in range(4):
            a1[c, pl.ds(to, R), :] = new[c] if c == 3 else new[c] + push * main_a[c, pl.ds(own, R), :]
        keep = pl.multiple_of(jnp.where(k == 0, 6, jnp.where(k == 5, 7, jnp.where(k < 3, k - 1, k + 1))) * R, 8)
        for n in range(7):
            cf[n, pl.ds(keep, R), :] = coefs[n]
        return 0

    lax.fori_loop(0, 6, plane, 0)
    for x, p in ((2, 3), (3, 4), (12, 5), (13, 6)):
        for c in range(4):
            a1[c, pl.ds(p * R, R), :] = a1_in[c, pl.ds(x * R, R), :]
    for x, p in ((2, 2), (13, 3)):
        for n in range(7):
            cf[n, pl.ds(p * R, R), :] = cf_in[n, pl.ds(x * R, R), :]
    for c in range(3):
        sent[c, pl.ds(0, T), :] = sa[c, pl.ds(R + 3, T), :]
        for k, p in ((1, 1), (2, 2), (3, 7), (4, 8)):
            sent[c, pl.ds(k * T, T), :] = a1[c, pl.ds(p * R + 3, T), :]
        sent[c, pl.ds(5 * T, T), :] = sa[c, pl.ds(8 * R + 3, T), :]
        sent[c, pl.ds(6 * T, T), :] = ea[c, pl.ds(2, T, stride=R), :]
        sent[c, pl.ds(7 * T, T), :] = ea[c, pl.ds(T + 3, T, stride=R), :]
    for k, n, row in ((0, 4, 3), (1, 3, T + 2)):
        beside[k, pl.ds(2, T - 4), :] = cf_in[n, pl.ds(2 * R + row, T - 4, stride=R), :]
        beside[k, pl.ds(0, 2), :] = cf[n, pl.ds(row, 2, stride=R), :]
        beside[k, pl.ds(T - 2, 2), :] = cf[n, pl.ds(4 * R + row, 2, stride=R), :]


def second_edges(w, a1, cf, part):
    ones_p, ones_m = edges_z(T)

    def plane(k, _):
        x = jnp.where(k < 3, k, k + 10)
        p = jnp.where(k < 3, k + 1, k + 3)
        second_plane(pl.multiple_of(x * T, 8), p * R + 3, k * R + 3, pl.multiple_of(k * T, 8), w, a1, cf, part, ones_p, ones_m)
        return 0

    lax.fori_loop(0, 6, plane, 0)


def finish(part, part_edges, cf, beside, inside, main_a, table, out):
    other = 1.0 - is_main()
    for x in range(T):
        k = x if x < 8 else x - 10
        rate = rate_rows(table, x, T) * other
        src, at = (part, x * T) if 3 <= x < T - 3 else (part_edges, k * T)
        new = [src[c, pl.ds(at, T), :] for c in range(4)]
        push, at = (inside, (x - 2) * T) if 2 <= x < T - 2 else (main_a, (x + 1 if x < 8 else x - 11) * T)
        for c in range(3):
            new[c] = new[c] + rate * push[c, pl.ds(at, T), :]
        if x in (0, T - 1):
            p, n, sign = (0, 2, -1.0) if x == 0 else (5, 1, 1.0)
            rate = rate_rows(table, -1 if x == 0 else T, T) * other
            pushed = [rate * main_a[c, pl.ds(p * T, T), :] for c in range(3)]
            coef = cf[n, pl.ds(k * R + 3, T), :]
            for c in range(3):
                new[c] = new[c] + coef * pushed[c]
            new[3] = new[3] + (sign * HALF) * pushed[0]
        for c in range(4):
            out[c, pl.ds(x * T, T), :] = new[c]
    rate = table[pl.ds(1, T), :] * other
    for k, y, sign in ((0, 0, -1.0), (1, T - 1, 1.0)):
        pushed = [rate * main_a[c, pl.ds((6 + k) * T, T), :] for c in range(3)]
        row = pl.ds(y, T, stride=T)
        for c in range(3):
            out[c, row, :] = out[c, row, :] + beside[k] * pushed[c]
        out[3, row, :] = out[3, row, :] + (sign * HALF) * pushed[1]


def ring(axis, by):
    devices = lax.axis_size(axis)
    return [(i, (i + by) % devices) for i in range(devices)]


def exchange(first, second, axis):
    first = lax.ppermute(first, axis, ring(axis, 1))
    second = lax.ppermute(second, axis, ring(axis, -1))
    return first, second


def on_device(wind, adjoint, turbines, fringe_range):
    y_msg, x_msg = shape(Y_LEN, T, NZ), shape(X_LEN, NZ)
    tile = shape(4, T * T, NZ)
    y1, y2, w, a, t = call(
        pack_y,
        (y_msg, y_msg, shape(3, T * T, NZ), tile, jax.ShapeDtypeStruct((T * T, NZ), jnp.int32)),
        [HBM] * 3,
        scratch=[pltpu.SemaphoreType.DMA((3,))],
    )(
        *(
            pltpu.with_memory_space_constraint(v, pltpu.HBM)
            for v in (wind.reshape(3, T * T, NZ), adjoint.reshape(4, T * T, NZ), turbines.reshape(T * T, NZ))
        )
    )
    y1, y2 = exchange(y1, y2, "gy")
    main_a = lax.ppermute(a, "dom", [(0, 1)])
    x1, x2 = call(
        pack_x,
        (x_msg, x_msg),
        [VMEM] * 5,
        scratch=[scratch(*planes(6, 3)), scratch(*planes(6, 4)), scratch(*planes(6))],
    )(w, a, t, y1, y2)
    x1, x2 = exchange(x1, x2, "gx")
    ew, ea, ed, vel = call(
        spread_rows,
        (shape(*planes(T, 3)), shape(*planes(T, 4)), shape(*planes(T)), shape(3, T * R, NZ)),
        [VMEM] * 6,
        flops=10**6,
    )(w, a, t, y1, y2, main_a)
    nu, cf, a1, part, table, inside = call(
        inner,
        (shape(*planes(T)), shape(*planes(T, 7)), shape(*planes(T, 4)), tile, shape(R, NZ), shape(3, (T - 4) * T, NZ)),
        [VMEM] * 5 + [SMEM],
        flops=10**7,
    )(w, ew, ea, ed, vel, fringe_range)
    inside = lax.ppermute(inside, "dom", [(0, 1)])
    cf_edges, a1_edges, sent, beside = call(
        edges,
        (shape(*planes(8, 7)), shape(*planes(10, 4)), shape(3, 8 * T, NZ), shape(2, T, NZ)),
        [VMEM] * 10,
        scratch=[scratch(*planes(10, 3)), scratch(*planes(10, 4)), scratch(*planes(10)), scratch(*planes(10))],
    )(x1, x2, ew, ea, ed, nu, vel, table, cf, a1)
    main_a1 = lax.ppermute(sent, "dom", [(0, 1)])
    part_edges = call(second_edges, shape(4, 6 * T, NZ), [VMEM] * 3, flops=10**6)(w, a1_edges, cf_edges)
    out = call(finish, tile, [VMEM] * 7)(part, part_edges, cf_edges, beside, inside, main_a1, table)
    return out.reshape(1, 4, T, T, NZ)


def solution(mesh):
    in_specs = (
        P("dom", None, "gx", "gy", None),
        P("dom", None, "gx", "gy", None),
        P("gx", "gy", None),
        P(),
    )
    out_specs = P("dom", None, "gx", "gy", None)
    return jax.shard_map(on_device, mesh=mesh, in_specs=in_specs, out_specs=out_specs, check_vma=False)
```
